256 devices in a mesh: ctx: 128 (over x, y, z), pipe: 2 (over core).
Axes of the slice: x: 4, y: 4, z: 8, core: 2. Of those that a mesh axis runs over, the one named last changes fastest.
Arguments:
- loaded: bfloat16 [2, 256, 128, 4096], P('pipe', 'ctx'), may hold values from -6 to 6
- counts: int32 [128], P('ctx'), may hold values from 0 to 2, as said below
- destinations: int32 [256], P('ctx'), may hold values from -1 to 127, as said below
- bounds: int32 [128], replicated, may hold values from 0 to 128, as said below
- se_gate: bfloat16 [2, 16384, 4096], P('pipe', 'ctx'), may hold values from -6 to 6
- mr_gate: bfloat16 [2, 16384, 4096], P('pipe', 'ctx'), may hold values from -6 to 6
- phase_grads: bfloat16 [2, 16384, 4096], P('pipe', 'ctx'), may hold values from -6 to 6
- se_taps: float32 [2, 256, 7], P('pipe'), may hold values from -2.5 to 2.5
- mr_taps: float32 [2, 256, 128], P('pipe'), may hold values from -0.5 to 0.5
Outputs:
- grad_input: bfloat16 [2, 16384, 4096], P('pipe', 'ctx')
- grad_se_gate: bfloat16 [2, 16384, 4096], P('pipe', 'ctx')
- grad_mr_gate: bfloat16 [2, 16384, 4096], P('pipe', 'ctx')
- grad_se_taps: float32 [2, 256, 7], P('pipe')
- grad_mr_taps: float32 [2, 256, 128], P('pipe')
The draws below stay inside these ranges and needn't reach their ends.
Inputs may be any that keep to these rules, and one draw needn't show every extreme that they name: `counts`: loaders hold 0 to 2 tiles, 128 in all; taken loader by loader and slot by slot they are the sequence's tiles in order, and loader i's first tile is tile i or i + 1. The first loader holds 2 and the last holds none. `destinations`: entry 2 i + j is the sequence tile held in slot j of loader i, and -1 where j is not below that loader's count. `bounds`: entry t is the offset within tile t at which a new segment starts, at most one a tile, or 128 where none starts; tile 0's is 0 and the last tile's is 128.
All inputs are finite; a program needn't handle non-finite values.
Results may differ from the reference program's by a relative error of at most 0.0085.
Values may be sent and summed in bfloat16 or wider, within the bound.
A program may use at most 192 MiB of HBM per device.

```python
import math
import jax
import jax.numpy as jnp
from jax import lax

CHANNELS = 4096
TILE = 128
SE_TAPS = 7
MR_TAPS = 128
GROUP = 16
TILES = 128
SLOTS = 256
TOKENS = 16384
GROUPS = 256


def route_plan(key):
    drift_bits = jax.random.randint(jax.random.fold_in(key, 11), (TILES + 1,), 0, 2)
    positions = jnp.arange(TILES + 1)
    drift_bits = jnp.where(positions == 0, 0, jnp.where(positions == TILES, 0, jnp.where(positions == 1, 1, jnp.where(positions == TILES - 1, 1, drift_bits))))
    held = 1 + drift_bits[1:] - drift_bits[:-1]
    return (drift_bits, held)


def draw_counts(key, part):
    drift_bits, held = route_plan(key)
    return held.astype(jnp.int32)


def draw_destinations(key, part):
    drift_bits, held = route_plan(key)
    loader = jnp.arange(TILES)
    first_tile = loader + drift_bits[:-1]
    paired = jnp.stack([first_tile, first_tile + 1], axis=1)
    living = jnp.arange(2)[None, :] < held[:, None]
    return jnp.where(living, paired, -1).reshape(-1).astype(jnp.int32)


def draw_bounds(key, part):
    cut_key = jax.random.fold_in(key, 23)
    none_key = jax.random.fold_in(key, 29)
    cut_at = jax.random.randint(cut_key, (TILES,), 0, TILE)
    without = jax.random.randint(none_key, (TILES,), 0, 2)
    offsets = jnp.where(without == 1, TILE, cut_at)
    positions = jnp.arange(TILES)
    offsets = jnp.where(positions == 0, 0, jnp.where(positions == TILES - 1, TILE, offsets))
    return offsets.astype(jnp.int32)


def level_of(rng, extent, split, smallest, largest):
    def one(position, shards_of):
        draws = jax.random.uniform(jax.random.fold_in(jax.random.fold_in(rng, 6), position), (shards_of,), jnp.float32, smallest / len(split), largest / len(split))
        return jnp.repeat(jnp.exp(draws), extent[position] // shards_of).reshape((-1,) + (1,) * (len(extent) - position - 1))

    loudness = one(*split[0])
    for cut in split[1:]:
        loudness = loudness * one(*cut)
    return loudness


def normal_values(rng, shape, deviation, bound, split=(), held_as=jnp.bfloat16):
    drawn = jax.random.normal(rng, shape, jnp.float32) * deviation
    if len(split) > 0:
        drawn = level_of(rng, shape, split, -0.22, 0.18) * drawn
    return jnp.clip(drawn, min=-bound, max=bound).astype(held_as)


def setup_inputs(seed: int = 0) -> dict:
    seeds = jax.random.split(jax.random.key(seed), 10)
    return {
        "loaded": normal_values(seeds[0], (2, SLOTS, TILE, CHANNELS), 1.0, 6.0, ((0, 2), (1, 128))),
        "counts": draw_counts(jax.random.fold_in(seeds[9], 71), 0),
        "destinations": draw_destinations(jax.random.fold_in(seeds[9], 71), 0),
        "bounds": draw_bounds(jax.random.fold_in(seeds[9], 71), 0),
        "se_gate": normal_values(seeds[4], (2, TOKENS, CHANNELS), 1.0, 6.0, ((0, 2), (1, 128))),
        "mr_gate": normal_values(seeds[5], (2, TOKENS, CHANNELS), 1.0, 6.0, ((0, 2), (1, 128))),
        "phase_grads": normal_values(seeds[6], (2, TOKENS, CHANNELS), 1.0, 6.0, ((0, 2), (1, 128))),
        "se_taps": normal_values(seeds[7], (2, GROUPS, SE_TAPS), 0.4, 2.5, ((0, 2),), jnp.float32),
        "mr_taps": normal_values(seeds[8], (2, GROUPS, MR_TAPS), 0.09, 0.5, ((0, 2),), jnp.float32),
    }


def toeplitz_rows(tap_table, starts):
    group_count = tap_table.shape[0]
    tap_count = tap_table.shape[1]
    row_count = starts.shape[0]
    col_count = 2 * tap_count
    tap_line = jnp.concatenate([jnp.zeros((group_count, 1), tap_table.dtype), tap_table[:, ::-1], jnp.zeros((group_count, col_count - tap_count), tap_table.dtype)], axis=1)
    spread_rows = jnp.broadcast_to(tap_line[:, None, :], (group_count, row_count, col_count + 1)).reshape(group_count, row_count * (col_count + 1))
    toeplitz = spread_rows[:, :row_count * col_count].reshape(group_count, row_count, col_count)
    columns = jnp.arange(col_count, dtype=jnp.int32)
    keep_mask = columns[None, :] - tap_count >= starts[:, None]
    return (jnp.where(keep_mask[None], toeplitz, jnp.zeros((), tap_table.dtype)), keep_mask)

def tap_sums(products):
    group_count = products.shape[0]
    row_count = products.shape[1]
    col_count = products.shape[2]
    flat = products.reshape(group_count, row_count * col_count)
    flat = jnp.pad(flat, ((0, 0), (0, row_count)))
    lagged = flat.reshape(group_count, row_count, col_count + 1)
    return lax.optimization_barrier(jnp.sum(lagged[:, :, 1:row_count + 1], axis=1))[:, ::-1]

def lag_grads(weighted, extended, keep_mask):
    pieces = 4
    row_count = weighted.shape[0]
    left_part = weighted.reshape(row_count, pieces, -1).transpose(1, 0, 2)
    right_part = extended.reshape(extended.shape[0], pieces, -1).transpose(1, 0, 2)

    def block_taps(operand_pair):
        front_part, back_part = operand_pair
        block_groups = front_part.shape[1] // GROUP
        products = jnp.einsum('rgc,sgc->grs', front_part.reshape(row_count, block_groups, GROUP), back_part.reshape(back_part.shape[0], block_groups, GROUP), preferred_element_type=jnp.float32)
        products = jnp.where(keep_mask[None], products, 0.0)
        return tap_sums(products)
    return lax.map(block_taps, (left_part, right_part)).reshape(-1, row_count)

def short_forward(extended, tap_table, starts):
    row_count = starts.shape[0]
    lead_rows = extended.shape[0] - row_count
    channel_taps = jnp.repeat(tap_table, GROUP, axis=0)
    positions = jnp.arange(row_count, dtype=jnp.int32)
    running = jnp.zeros((row_count, extended.shape[1]), jnp.float32)
    for offset in range(tap_table.shape[1]):
        shifted = extended[lead_rows - offset:lead_rows - offset + row_count].astype(jnp.float32)
        allowed = (positions - offset >= starts)[:, None]
        running = running + jnp.where(allowed, channel_taps[:, offset][None, :] * shifted, 0.0)
    return running

def short_back(extended, tap_table, starts_ext):
    row_count = extended.shape[0] - 8
    channel_taps = jnp.repeat(tap_table, GROUP, axis=0)
    positions = jnp.arange(row_count, dtype=jnp.int32)
    running = jnp.zeros((row_count, extended.shape[1]), jnp.float32)
    for offset in range(tap_table.shape[1]):
        shifted = extended[offset:offset + row_count].astype(jnp.float32)
        allowed = (positions >= starts_ext[offset:offset + row_count])[:, None]
        running = running + jnp.where(allowed, channel_taps[:, offset][None, :] * shifted, 0.0)
    return running

def short_taps_grad(weighted, extended, tap_table, starts):
    row_count = starts.shape[0]
    lead_rows = extended.shape[0] - row_count
    positions = jnp.arange(row_count, dtype=jnp.int32)
    weighted_f = weighted.astype(jnp.float32)
    columns = []
    for offset in range(tap_table.shape[1]):
        shifted = extended[lead_rows - offset:lead_rows - offset + row_count].astype(jnp.float32)
        allowed = (positions - offset >= starts)[:, None]
        summed = lax.optimization_barrier(jnp.sum(jnp.where(allowed, weighted_f * shifted, 0.0), axis=0))
        columns.append(lax.optimization_barrier(jnp.sum(summed.reshape(-1, GROUP), axis=1)))
    return jnp.stack(columns, axis=1)

def seq_starts(bounds):
    tile_count = bounds.shape[0]
    positions = jnp.arange(tile_count * TILE, dtype=jnp.int32)
    tile_of = positions // TILE
    within = positions - tile_of * TILE
    mine = bounds[tile_of]
    marker = jnp.where(within >= mine, tile_of * TILE + mine, -1000000).astype(jnp.int32)
    return lax.cummax(marker, axis=0)

def phase_backward(layer_input, gate_se, gate_mr, incoming, taps_se, taps_mr, starts):
    length = layer_input.shape[0]
    tile_count = length // TILE
    group_count = CHANNELS // GROUP
    scale = 1.0 / math.sqrt(length * GROUP)
    rim_rows = 8
    padded_input = jnp.pad(layer_input, ((rim_rows, 0), (0, 0)))
    se_mix = short_forward(padded_input, taps_se, starts)
    mid_acts = (layer_input.astype(jnp.float32) + gate_se.astype(jnp.float32) * se_mix).astype(jnp.bfloat16)
    taps_low = taps_mr.astype(jnp.bfloat16)
    mid_pad = jnp.pad(mid_acts, ((TILE, 0), (0, 0)))
    weighted = (gate_mr.astype(jnp.float32) * incoming.astype(jnp.float32)).astype(jnp.bfloat16)
    tile_ids = jnp.arange(tile_count, dtype=jnp.int32)

    def tile_parts(tile_num):
        anchor = tile_num * TILE
        extended = lax.dynamic_slice_in_dim(mid_pad, anchor, 2 * TILE, 0).astype(jnp.float32)
        relative = lax.dynamic_slice_in_dim(starts, anchor, TILE, 0) - anchor
        matrix, keep_mask = toeplitz_rows(taps_low, relative)
        return (anchor, extended, matrix.astype(jnp.float32), keep_mask)

    def forward_tile(tile_num):
        anchor, extended, matrix, keep_mask = tile_parts(tile_num)
        return jnp.einsum('grs,sgc->rgc', matrix, extended.reshape(2 * TILE, group_count, GROUP)).reshape(TILE, CHANNELS)
    mr_mix = lax.map(forward_tile, tile_ids).reshape(length, CHANNELS)
    grad_gate_mr = (incoming.astype(jnp.float32) * mr_mix).astype(jnp.bfloat16)

    def back_tile(tile_num):
        anchor, extended, matrix, keep_mask = tile_parts(tile_num)
        local = lax.dynamic_slice_in_dim(weighted, anchor, TILE, 0).astype(jnp.float32)
        grouped = local.reshape(TILE, group_count, GROUP)
        own_part = jnp.einsum('grs,rgc->sgc', matrix[:, :, TILE:], grouped).reshape(TILE, CHANNELS)
        prior_part = jnp.einsum('grs,rgc->sgc', matrix[:, :, :TILE], grouped).reshape(TILE, CHANNELS)
        return (own_part, prior_part, lag_grads(local, extended, keep_mask))
    own_all, prior_all, taps_all = lax.map(back_tile, tile_ids)
    prior_moved = jnp.concatenate([prior_all[1:], jnp.zeros((1, TILE, CHANNELS), jnp.float32)], axis=0)
    grad_mid = (incoming.astype(jnp.float32) + own_all.reshape(length, CHANNELS) + prior_moved.reshape(length, CHANNELS)).astype(jnp.bfloat16)
    mr_grad = lax.optimization_barrier(jnp.sum(taps_all, axis=0)) * scale
    grad_gate_se = (grad_mid.astype(jnp.float32) * se_mix).astype(jnp.bfloat16)
    weighted_se = (gate_se.astype(jnp.float32) * grad_mid.astype(jnp.float32)).astype(jnp.bfloat16)
    after_pad = jnp.pad(weighted_se, ((0, rim_rows), (0, 0)))
    starts_ext = jnp.concatenate([starts, jnp.full((rim_rows,), 2 ** 30, jnp.int32)])
    grad_x = (grad_mid.astype(jnp.float32) + short_back(after_pad, taps_se, starts_ext)).astype(jnp.bfloat16)
    se_grad = short_taps_grad(weighted_se, padded_input, taps_se, starts) * scale
    return (grad_x, grad_gate_se, grad_gate_mr, se_grad, mr_grad)

def reference(loaded, counts, destinations, bounds, se_gate, mr_gate, phase_grads, se_taps, mr_taps):
    tile_count = counts.shape[0]
    slot_ids = jnp.arange(2 * tile_count, dtype=jnp.int32)
    holding = slot_ids % 2 < counts[slot_ids // 2]
    target = jnp.where(holding, destinations, tile_count).astype(jnp.int32)
    placed = jnp.zeros((2, tile_count + 1, TILE, CHANNELS), jnp.bfloat16).at[:, target].set(loaded)
    inputs = placed[:, :tile_count].reshape(2, tile_count * TILE, CHANNELS)
    starts = seq_starts(bounds)
    results = [phase_backward(inputs[phase_id], se_gate[phase_id], mr_gate[phase_id], phase_grads[1 - phase_id], se_taps[phase_id], mr_taps[phase_id], starts) for phase_id in range(2)]
    grad_input = jnp.stack([results[0][0], results[1][0]])
    grad_se_gate = jnp.stack([results[0][1], results[1][1]])
    grad_mr_gate = jnp.stack([results[0][2], results[1][2]])
    grad_se_taps = jnp.stack([results[0][3], results[1][3]])
    grad_mr_taps = jnp.stack([results[0][4], results[1][4]])
    return (grad_input, grad_se_gate, grad_mr_gate, grad_se_taps, grad_mr_taps)
```

```python
import functools
import math

import jax
import jax.numpy as jnp
from jax import lax
from jax.experimental import pallas as pl
from jax.experimental.pallas import tpu as pltpu
from jax.sharding import PartitionSpec as P

GROUP = 16
ROWS = 128
LANES = 128
WIDE = 512
RIM = 8
BLOCK_GROUPS = LANES // GROUP
F32 = jnp.float32
BF16 = jnp.bfloat16
NT = (((1,), (1,)), ((), ()))


def iotas():
    row = lax.broadcasted_iota(jnp.int32, (ROWS, LANES), 0)
    col = lax.broadcasted_iota(jnp.int32, (ROWS, LANES), 1)
    return row, col


def pipelined(kernel, width, out_shape, in_specs, out_specs, scratch, flops, moved):
    return pl.pallas_call(
        kernel,
        grid_spec=pltpu.PrefetchScalarGridSpec(
            num_scalar_prefetch=1,
            grid=(width // min(WIDE, width),),
            in_specs=in_specs,
            out_specs=out_specs,
            scratch_shapes=scratch,
        ),
        out_shape=out_shape,
        compiler_params=pltpu.CompilerParams(
            dimension_semantics=("arbitrary",), vmem_limit_bytes=48 << 20
        ),
        cost_estimate=pl.CostEstimate(flops=flops, bytes_accessed=moved, transcendentals=0),
    )


def cols(rows, width):
    return pl.BlockSpec((rows, min(WIDE, width)), lambda i, s: (0, i))


def mats(width):
    return pl.BlockSpec((min(WIDE, width) // GROUP, ROWS, LANES), lambda i, s: (i, 0, 0))


def lane_blocks(body, width):
    def step(j, carry):
        body(j, pl.ds(pl.multiple_of(j * LANES, LANES), LANES))
        return carry

    lax.fori_loop(0, min(WIDE, width) // LANES, step, 0)


def distances(s):
    row, _ = iotas()
    bound, before = s[0], s[1]
    start = jnp.where(row >= bound, bound, jnp.where(before < ROWS, before - ROWS, -1000000))
    return row - start


def fill_short_masks(s, mask_ref, taps):
    @pl.when(pl.program_id(0) == 0)
    def _():
        away = distances(s)
        for k in range(taps):
            mask_ref[k] = jnp.where(away >= k, 1.0, 0.0).astype(F32)


def circulant_kernel(s, taps_ref, turned_ref, fore_ref, back_ref):
    def one(g, carry):
        a = jnp.broadcast_to(turned_ref[pl.ds(g, 1), :], (ROWS, LANES))
        fore_ref[g] = pltpu.roll(a, 0, 1, stride=1, stride_axis=0).astype(BF16)
        b = jnp.broadcast_to(taps_ref[pl.ds(g, 1), :], (ROWS, LANES))
        back_ref[g] = pltpu.roll(b, 0, 1, stride=1, stride_axis=0).astype(BF16)
        return carry

    lax.fori_loop(0, taps_ref.shape[0], one, 0)


def circulants(scalars, taps_low, width):
    groups = width // GROUP
    turned = jnp.roll(taps_low[:, ::-1], 1, axis=1)
    per = min(WIDE, width) // GROUP
    spec = pl.BlockSpec((per, LANES), lambda i, s: (i, 0))
    shape = jax.ShapeDtypeStruct((groups, ROWS, LANES), BF16)
    return pipelined(
        circulant_kernel, width, (shape, shape), [spec, spec], (mats(width), mats(width)), [],
        0, groups * ROWS * LANES * 4,
    )(scalars, taps_low, turned)


def mid_kernel(taps, s, slot_ref, came_ref, rows_ref, gate_ref, tap_ref,
               input_ref, mix_ref, mid_ref, mask_ref, line_ref):
    fill_short_masks(s, mask_ref, taps)
    held = s[3] > 0

    def body(j, at):
        x16 = jnp.where(held, slot_ref[:, at], came_ref[:, at])
        x = x16.astype(F32)
        line_ref[:RIM] = rows_ref[:, at].astype(F32)
        line_ref[RIM:] = x
        mix = jnp.zeros((ROWS, LANES), F32)
        for k in range(taps):
            mix += line_ref[RIM - k : RIM - k + ROWS] * mask_ref[k] * tap_ref[k : k + 1, at]
        input_ref[:, at] = x16
        mix_ref[:, at] = mix
        mid_ref[:, at] = (x + gate_ref[:, at].astype(F32) * mix).astype(BF16)

    lane_blocks(body, slot_ref.shape[1])


def back_kernel(taps, s, fore_ref, next_ref, mid_ref, mat_ref, grad_ref, mix_ref, gate_ref,
                input_ref, rows_ref,
                gmid_ref, ggate_ref, wse_ref, lag_ref, short_ref,
                mask_ref, line_ref, pair_ref):
    fill_short_masks(s, mask_ref, taps)
    step = pl.program_id(0)
    bound, after = s[0], s[2]
    row, col = iotas()
    own_keep = (row <= col) & ((col < bound) | (row >= bound))
    next_keep = (row > col) & (col < after) & ((bound >= ROWS) | (row >= bound))
    turn = (ROWS - 1) - row
    upper = turn <= col
    any_keep = (upper & ((col < bound) | (turn >= bound))) | (
        (turn > col) & (col < after) & ((bound >= ROWS) | (turn >= bound))
    )
    flip = jnp.where(turn == col, 1.0, 0.0).astype(BF16)
    lane_group = lax.broadcasted_iota(jnp.int32, (1, LANES), 1) // GROUP

    @pl.when(step == 0)
    def _():
        short_ref[...] = jnp.zeros_like(short_ref)

    def body(j, at):
        pair_ref[:ROWS] = fore_ref[:, at]
        pair_ref[ROWS:] = next_ref[:, at]
        pair = pair_ref[...]
        mid = jnp.dot(flip, mid_ref[:, at], preferred_element_type=F32).astype(BF16)
        total = jnp.zeros((ROWS, LANES), F32)
        for g in range(BLOCK_GROUPS):
            mine = lane_group == g
            d = mat_ref[j * BLOCK_GROUPS + g]
            zero = jnp.zeros_like(d)
            lhs = jnp.concatenate(
                [jnp.where(own_keep, d, zero), jnp.where(next_keep, d, zero)], axis=1
            )
            y = jnp.dot(lhs, pair, preferred_element_type=F32)
            total = jnp.where(mine, y, total)
            z = lax.dot_general(
                jnp.where(mine, mid, jnp.zeros_like(mid)), pair, NT, preferred_element_type=F32
            )
            z = jnp.where(upper, z[:, :LANES], z[:, LANES:])
            z = jnp.where(any_keep, z, 0.0)
            z = pltpu.roll(z, 1, 1, stride=1, stride_axis=0)
            lag_ref[pl.ds(j * BLOCK_GROUPS + g, 1), :] = jnp.sum(z, axis=0, keepdims=True)
        gmid16 = (grad_ref[:, at].astype(F32) + total).astype(BF16)
        gmid = gmid16.astype(F32)
        gmid_ref[:, at] = gmid16
        ggate_ref[:, at] = (gmid * mix_ref[:, at]).astype(BF16)
        wse16 = (gate_ref[:, at].astype(F32) * gmid).astype(BF16)
        wse_ref[:, at] = wse16
        wse = wse16.astype(F32)
        line_ref[:RIM] = rows_ref[:, at].astype(F32)
        line_ref[RIM:] = input_ref[:, at].astype(F32)
        parts = []
        for k in range(taps):
            prod = line_ref[RIM - k : RIM - k + ROWS] * mask_ref[k] * wse
            parts.append(jnp.sum(prod, axis=0, keepdims=True))
        parts.append(jnp.zeros((RIM - taps, LANES), F32))
        lanes = jnp.concatenate(parts, axis=0)
        groups = short_ref.shape[1]
        where_l = lax.broadcasted_iota(jnp.int32, (LANES, groups), 0) // GROUP
        where_g = lax.broadcasted_iota(jnp.int32, (LANES, groups), 1)
        first = step * (fore_ref.shape[1] // GROUP) + j * BLOCK_GROUPS
        pick = jnp.where(where_g == where_l + first, 1.0, 0.0).astype(F32)
        short_ref[...] += jnp.dot(
            lanes, pick, preferred_element_type=F32, precision=lax.Precision.HIGHEST
        )

    lane_blocks(body, fore_ref.shape[1])


def input_kernel(taps, s, wse_ref, after_ref, gmid_ref, tap_ref, out_ref, mask_ref, line_ref):
    @pl.when(pl.program_id(0) == 0)
    def _():
        away = distances(s)
        row, _ = iotas()
        bound, after = s[0], s[2]
        for k in range(taps):
            inside = jnp.where(away >= k, 1.0, 0.0).astype(F32)
            mask_ref[k, :ROWS] = inside
            rim = lax.broadcasted_iota(jnp.int32, (RIM, LANES), 0)
            start = jnp.where(
                rim >= after, after, jnp.where(bound < ROWS, bound - ROWS, -1000000)
            )
            mask_ref[k, ROWS:] = jnp.where(rim - start >= k, 1.0, 0.0).astype(F32)

    def body(j, at):
        line_ref[:ROWS] = wse_ref[:, at].astype(F32)
        line_ref[ROWS:] = after_ref[:, at].astype(F32)
        total = gmid_ref[:, at].astype(F32)
        back = jnp.zeros((ROWS, LANES), F32)
        for k in range(taps):
            back += line_ref[k : k + ROWS] * mask_ref[k, k : k + ROWS] * tap_ref[k : k + 1, at]
        out_ref[:, at] = (total + back).astype(BF16)

    lane_blocks(body, wse_ref.shape[1])


def mix_kernel(s, mid_ref, prior_ref, mat_ref, grad_ref, out_ref, pair_ref):
    bound, before = s[0], s[1]
    row, col = iotas()
    own_keep = (col <= row) & ((row < bound) | (col >= bound))
    prior_keep = (col > row) & (row < bound) & ((before >= ROWS) | (col >= before))
    lane_group = lax.broadcasted_iota(jnp.int32, (1, LANES), 1) // GROUP

    def body(j, at):
        pair_ref[:ROWS] = mid_ref[:, at]
        pair_ref[ROWS:] = prior_ref[:, at]
        pair = pair_ref[...]
        total = jnp.zeros((ROWS, LANES), F32)
        for g in range(BLOCK_GROUPS):
            c = mat_ref[j * BLOCK_GROUPS + g]
            zero = jnp.zeros_like(c)
            lhs = jnp.concatenate(
                [jnp.where(own_keep, c, zero), jnp.where(prior_keep, c, zero)], axis=1
            )
            y = jnp.dot(lhs, pair, preferred_element_type=F32)
            total = jnp.where(lane_group == g, y, total)
        out_ref[:, at] = (grad_ref[:, at].astype(F32) * total).astype(BF16)

    lane_blocks(body, mid_ref.shape[1])


def moved(block, axis, distance):
    size = lax.axis_size(axis)
    route = [(i, i + distance) for i in range(size) if 0 <= i + distance < size]
    return lax.ppermute(block, axis, route)


def body(loaded, counts, destinations, bounds, se_gate, mr_gate, phase_grads, se_taps, mr_taps):
    ctx_count = lax.axis_size("ctx")
    shard = lax.axis_index("ctx")
    slots = loaded[0]
    width = slots.shape[2]
    groups = width // GROUP
    taps = se_taps.shape[2]
    held = counts[0]
    own = (held >= 1) & (destinations[0] == shard)
    send_first = (held >= 1) & (destinations[0] == shard + 1)
    outgoing = jnp.where(send_first, slots[0], slots[1])
    arrived = moved(outgoing, "ctx", 1)
    incoming = lax.ppermute(phase_grads, "pipe", [(0, 1), (1, 0)])[0]
    nothing = jnp.zeros((RIM, width), BF16)
    sends = send_first | ((held >= 2) & (destinations[1] == shard + 1))
    near = moved(jnp.where(own, slots[0, ROWS - RIM :], nothing), "ctx", 1)
    far = moved(jnp.where(sends, outgoing[ROWS - RIM :], nothing), "ctx", 2)
    rows_before = near + far
    gate_se, gate_mr = se_gate[0], mr_gate[0]
    tile_total = bounds.shape[0]
    bound = bounds[shard]
    before = jnp.where(shard > 0, bounds[jnp.maximum(shard - 1, 0)], ROWS)
    after = jnp.where(
        shard + 1 < tile_total, bounds[jnp.minimum(shard + 1, tile_total - 1)], 0
    )
    scalars = jnp.stack([bound, before, after, own.astype(jnp.int32)]).astype(jnp.int32)
    weighted = (gate_mr.astype(F32) * incoming.astype(F32)).astype(BF16)
    weighted_next = moved(weighted, "ctx", -1)
    taps_low = mr_taps[0].astype(BF16).astype(F32)
    fore_mats, back_mats = circulants(scalars, taps_low, width)
    tap_lanes = jnp.repeat(jnp.pad(se_taps[0].T, ((0, RIM - taps), (0, 0))), GROUP, axis=1)

    wide16 = jax.ShapeDtypeStruct((ROWS, width), BF16)
    wide32 = jax.ShapeDtypeStruct((ROWS, width), F32)
    full, rim = cols(ROWS, width), cols(RIM, width)
    size = ROWS * width
    masks = pltpu.VMEM((taps, ROWS, LANES), F32)
    line = pltpu.VMEM((ROWS + RIM, LANES), F32)
    pair = pltpu.VMEM((2 * ROWS, LANES), BF16)
    layer_input, se_mix, mid = pipelined(
        functools.partial(mid_kernel, taps), width, (wide16, wide32, wide16),
        [full, full, rim, full, rim], (full, full, full), [masks, line],
        size * 40, size * 14,
    )(scalars, slots[0], arrived, rows_before, gate_se, tap_lanes)
    mid_prior = moved(mid, "ctx", 1)
    block_groups = min(WIDE, width) // GROUP
    gmid, ggate, wse, lag, short = pipelined(
        functools.partial(back_kernel, taps), width,
        (wide16, wide16, wide16, jax.ShapeDtypeStruct((groups, LANES), F32),
         jax.ShapeDtypeStruct((RIM, groups), F32)),
        [full, full, full, mats(width), full, full, full, full, rim],
        (full, full, full, pl.BlockSpec((block_groups, LANES), lambda i, s: (i, 0)),
         pl.BlockSpec((RIM, groups), lambda i, s: (0, 0))),
        [masks, line, pair],
        groups * ROWS * 256 * 512, size * 40,
    )(scalars, weighted, weighted_next, mid, back_mats, incoming, se_mix, gate_se, layer_input,
      rows_before)
    after_rows = moved(wse[:RIM], "ctx", -1)
    line_sum = jnp.concatenate([lag.reshape(-1), short.reshape(-1)])
    line_sum = lax.psum(line_sum, "ctx")
    (grad_x,) = pipelined(
        functools.partial(input_kernel, taps), width, (wide16,),
        [full, rim, full, rim], (full,),
        [pltpu.VMEM((taps, ROWS + RIM, LANES), F32), line],
        size * 40, size * 8,
    )(scalars, wse, after_rows, gmid, tap_lanes)
    (grad_gate_mr,) = pipelined(
        mix_kernel, width, (wide16,),
        [full, full, mats(width), full], (full,), [pair],
        groups * ROWS * 256 * 256, size * 24,
    )(scalars, mid, mid_prior, fore_mats, incoming)
    scale = 1.0 / math.sqrt(ctx_count * ROWS * GROUP)
    cut = groups * LANES
    mr_total = line_sum[:cut].reshape(groups, LANES) * scale
    se_total = line_sum[cut:].reshape(RIM, groups)[:taps].T * scale
    return grad_x[None], ggate[None], grad_gate_mr[None], se_total[None], mr_total[None]


def solution(mesh):
    return jax.shard_map(
        body,
        mesh=mesh,
        in_specs=(
            P("pipe", "ctx", None, None),
            P("ctx"),
            P("ctx"),
            P(),
            P("pipe", "ctx", None),
            P("pipe", "ctx", None),
            P("pipe", "ctx", None),
            P("pipe", None, None),
            P("pipe", None, None),
        ),
        out_specs=(
            P("pipe", "ctx", None),
            P("pipe", "ctx", None),
            P("pipe", "ctx", None),
            P("pipe", None, None),
            P("pipe", None, None),
        ),
        check_vma=False,
    )
```
